256 devices in a mesh: slide: 16 (over y, x), row: 4 (over z_hi, core), col: 4 (over z_lo).
Axes of the slice: x: 4, y: 4, z: 8 (z_hi: 2, z_lo: 4; z = z_hi * 4 + z_lo), core: 2. Of those that a mesh axis runs over, the one named last changes fastest.
Arguments:
- features: bfloat16 [16, 256, 512, 256], P('slide', 'row', 'col'), may hold values from -6 to 6
- out_grad: bfloat16 [16, 256, 512, 256], P('slide', 'row', 'col'), may hold values from -6 to 6
- depth_weight: bfloat16 [9, 256], replicated, may hold values from -2 to 2
- point_weight: bfloat16 [256, 256], P(('slide', 'row', 'col')), may hold values from -0.375 to 0.375
Outputs:
- feature_grad: bfloat16 [16, 256, 512, 256], P('slide', 'row', 'col')
- point_grad: float32 [256, 256], P(('slide', 'row', 'col'))
- depth_grad: float32 [9, 256], replicated
The draws below stay inside these ranges and needn't reach their ends.
All inputs are finite; a program needn't handle non-finite values.
Results may differ from the reference program's by a relative error of at most 0.007.
Values may be sent and summed in bfloat16 or wider, within the bound.
No kernel may reach another device: no remote copies, remote signals or barrier semaphores. Data moves between devices by JAX's collectives and lax.ppermute only.
A program may use at most 128 MiB of HBM per device.

```python
import math
import jax
import jax.numpy as jnp
from jax import lax

CHANNELS = 256
HH = 256
WW = 512
N_SLIDE = 16


def raised(entries, rng, source, target, blocks, factor):
    def block_of(position):
        return (jnp.arange(entries.shape[position]) // (entries.shape[position] // blocks)).reshape((-1,) + (1,) * (entries.ndim - 1 - position))

    one_side = jax.random.permutation(rng, blocks)[block_of(target)]
    second = (block_of(target) + blocks // 2) % blocks
    return jnp.where((block_of(source) == one_side) | (block_of(source) == second), factor * entries, entries)


def levels(own_key, shape, pieces, low, top_value):
    loudness = 1.0
    for dim, parts in pieces:
        heights = jax.random.uniform(jax.random.fold_in(jax.random.fold_in(own_key, 6), dim), (parts,), jnp.float32, low / len(pieces), top_value / len(pieces))
        loudness = loudness * jnp.repeat(jnp.exp(heights), shape[dim] // parts).reshape((-1,) + (1,) * (len(shape) - 1 - dim))
    return loudness


def gaussian(stream_key, shape, spread, most, pieces=(), dtype=jnp.bfloat16):
    drawn = spread * jax.random.normal(stream_key, shape, jnp.float32)
    if pieces:
        drawn = drawn * levels(stream_key, shape, pieces, -0.22, 0.18)
    return jnp.clip(drawn, -most, most).astype(dtype)


def noise_with(stream_key, shape, spread, most, split, heavy, dtype=jnp.bfloat16):
    result = spread * jax.random.normal(stream_key, shape, jnp.float32)
    if split:
        result = result * levels(stream_key, shape, split, -0.22, 0.18)
    return jnp.clip(raised(result, jax.random.fold_in(stream_key, 3), *heavy), -most, most).astype(dtype)


def setup_inputs(seed: int = 0) -> dict:
    splits = jax.random.split(jax.random.key(seed), 5)
    features = noise_with(splits[0], (N_SLIDE, HH, WW, CHANNELS), 1.0, 6.0, ((0, 16), (1, 4), (2, 4)), (0, 3, 16, 2.0))
    out_grad = gaussian(splits[1], (N_SLIDE, HH, WW, CHANNELS), 1.0, 6.0, ((0, 16), (1, 4), (2, 4)))
    depth_weight = gaussian(splits[2], (9, CHANNELS), 9 ** -0.5, 2.0)
    point_weight = gaussian(splits[3], (CHANNELS, CHANNELS), CHANNELS ** -0.5, 0.375, ((0, 256),))
    return dict(features=features, out_grad=out_grad, depth_weight=depth_weight, point_weight=point_weight)


def one_slide(args, depth_weight, point_weight):
    feat, grad = args
    rows, cols, chans = feat.shape
    taps = depth_weight.astype(jnp.float32)
    padded = jnp.pad(feat, ((2, 2), (2, 2), (0, 0))).astype(jnp.float32)
    mid = jnp.zeros((rows, cols, chans), jnp.float32)
    for a in range(3):
        for b in range(3):
            mid = mid + taps[a * 3 + b] * padded[2 * a:2 * a + rows, 2 * b:2 * b + cols]
    mid = mid.astype(jnp.bfloat16)
    grad_flat = grad.reshape(rows * cols, chans)
    mid_grad = jnp.dot(grad_flat, point_weight.T, preferred_element_type=jnp.float32).astype(jnp.bfloat16)
    mid_grad = mid_grad.reshape(rows, cols, chans)
    grad_pad = jnp.pad(mid_grad, ((2, 2), (2, 2), (0, 0))).astype(jnp.float32)
    back = jnp.zeros((rows, cols, chans), jnp.float32)
    for a in range(3):
        for b in range(3):
            back = back + taps[a * 3 + b] * grad_pad[4 - 2 * a:4 - 2 * a + rows, 4 - 2 * b:4 - 2 * b + cols]
    mid_f = mid_grad.astype(jnp.float32)
    tap_terms = []
    for a in range(3):
        for b in range(3):
            tap_terms.append(lax.optimization_barrier(jnp.sum(padded[2 * a:2 * a + rows, 2 * b:2 * b + cols] * mid_f, axis=(0, 1))))
    point_part = jnp.dot(mid.reshape(rows * cols, chans).T, grad_flat, preferred_element_type=jnp.float32)
    return (back.astype(jnp.bfloat16), point_part, jnp.stack(tap_terms))

def reference(features, out_grad, depth_weight, point_weight):
    scale = 1.0 / math.sqrt(N_SLIDE * HH * WW)
    feature_grad, point_parts, tap_parts = lax.map(lambda t: one_slide(t, depth_weight, point_weight), (features, out_grad))
    point_grad = lax.optimization_barrier(jnp.sum(point_parts, axis=0)) * scale
    depth_grad = lax.optimization_barrier(jnp.sum(tap_parts, axis=0)) * scale
    return (feature_grad, point_grad, depth_grad)
```

```python
import math

import jax
import jax.numpy as jnp
from jax import lax
from jax.experimental import pallas as pl
from jax.experimental.pallas import tpu as pltpu
from jax.sharding import PartitionSpec as P

BF16 = jnp.bfloat16
F32 = jnp.float32
IN_VMEM = pl.BlockSpec(memory_space=pltpu.VMEM)


def whole(body, outs, args, name, flops, limit, scratch=()):
    size = sum(math.prod(x.shape) * x.dtype.itemsize for x in (*args, *outs))
    return pl.pallas_call(
        body,
        out_shape=outs,
        in_specs=[IN_VMEM] * len(args),
        out_specs=[IN_VMEM] * len(outs),
        scratch_shapes=scratch,
        name=name,
        cost_estimate=pl.CostEstimate(
            flops=flops, bytes_accessed=size, transcendentals=0
        ),
        compiler_params=pltpu.CompilerParams(vmem_limit_bytes=limit << 20),
    )(*args)


def shifted(above, grad, below, left, right, out):
    rows, cols, chans = grad.shape

    def put(i, row):
        out[i, :, 0:chans] = jnp.concatenate([row[2:], right[i]], axis=0)
        out[i, :, chans : 2 * chans] = row
        out[i, :, 2 * chans : 3 * chans] = jnp.concatenate(
            [left[i], row[: cols - 2]], axis=0
        )

    for i in range(2):
        put(i, above[i])
        put(rows + 2 + i, below[i])
    lax.fori_loop(0, rows, lambda i, c: (put(i + 2, grad[i]), c)[1], 0)


def moments(feat, above, grad, below, left, right, moment, wide):
    rows, cols, chans = feat.shape
    step = 8
    shifted(above, grad, below, left, right, wide)
    moment[...] = jnp.zeros_like(moment)

    def body(t, c):
        first = pl.multiple_of(t * step, step)
        lhs = feat[pl.ds(first, step)].reshape(step * cols, chans)
        for a in range(3):
            rhs = wide[pl.ds(first + 4 - 2 * a, step)]
            moment[a] += lax.dot_general(
                lhs,
                rhs.reshape(step * cols, 3 * chans),
                (((0,), (0,)), ((), ())),
                preferred_element_type=F32,
            )
        return c

    lax.fori_loop(0, rows // step, body, 0)


def finish(moment, point, taps, out):
    chans = point.shape[0]
    p = point[...].astype(F32)
    acc = jnp.zeros((chans, chans), F32)
    lane = lax.broadcasted_iota(jnp.int32, (chans, 128), 1)
    sums = jnp.zeros((chans, 128), F32)
    for a in range(3):
        for b in range(3):
            k = 3 * a + b
            m = moment[a, :, b * chans : (b + 1) * chans]
            acc = acc + taps[:, k : k + 1] * m
            sums = jnp.where(lane == k, jnp.sum(p * m, axis=1, keepdims=True), sums)
    groups = out.shape[0]
    share = chans // groups
    tap_rows = sums.T[:16]
    for s in range(groups):
        out[s, :share] = acc[s * share : (s + 1) * share]
        out[s, share:] = tap_rows


def second(got, out):
    total = got[0]
    for s in range(1, got.shape[0]):
        total = total + got[s]
    rows = total.shape[0] // 2
    tap = total[rows:]
    sub = lax.broadcasted_iota(jnp.int32, tap.shape, 0)
    for r in range(out.shape[0]):
        out[r] = jnp.where(sub == 9, total[r : r + 1], tap)


def third(scale, got, taps, row):
    total = got[0]
    for s in range(1, got.shape[0]):
        total = total + got[s]
    total = total * scale
    taps[...] = total[:9]
    row[...] = total[9:10]


def back(above, grad, below, left, right, point, taps, out, wide, weights):
    rows, cols, chans = grad.shape
    step = 8
    p = point[...].astype(F32)
    for k in range(9):
        weights[k // 3, :, (k % 3) * chans : (k % 3 + 1) * chans] = (
            p * taps[:, k : k + 1]
        ).astype(BF16)
    shifted(above, grad, below, left, right, wide)

    def body(t, c):
        first = pl.multiple_of(t * step, step)
        acc = jnp.zeros((step * cols, chans), F32)
        for a in range(3):
            lhs = wide[pl.ds(first + 4 - 2 * a, step)]
            acc = acc + lax.dot_general(
                lhs.reshape(step * cols, 3 * chans),
                weights[a],
                (((1,), (1,)), ((), ())),
                preferred_element_type=F32,
            )
        out[pl.ds(first, step)] = acc.reshape(step, cols, chans).astype(BF16)
        return c

    lax.fori_loop(0, rows // step, body, 0)


def spread(x, axes):
    count = lax.axis_size(axes)
    return lax.all_to_all(
        jnp.broadcast_to(x[None], (count, *x.shape)), axes, 0, 0, tiled=True
    )


def moved(x, axis, by):
    count = lax.axis_size(axis)
    pairs = [(i, i + by) for i in range(count) if 0 <= i + by < count]
    return lax.ppermute(x, axis, pairs)


def on_device(features, out_grad, depth_weight, point_weight):
    feat, grad = features[0], out_grad[0]
    rows, cols, chans = feat.shape
    place = ("row", "col")
    slides = lax.axis_size("slide")
    scale = 1.0 / math.sqrt(slides * lax.axis_size(place) * rows * cols)
    taps = depth_weight.astype(F32).T

    above = moved(grad[rows - 2 :], "row", 1)
    below = moved(grad[:2], "row", -1)
    block = spread(point_weight, place).reshape(-1, chans)
    ends = [
        jnp.concatenate([x[:, s] for x in (above, grad, below)], axis=0)
        for s in (slice(cols - 2, None), slice(0, 2))
    ]
    left = moved(ends[0], "col", 1)
    right = moved(ends[1], "col", -1)
    point = spread(block, "slide").reshape(-1, chans)

    halo = (above, grad, below, left, right)
    macs = rows * cols * chans * chans
    wide = pltpu.VMEM((rows + 4, cols, 3 * chans), BF16)
    (moment,) = whole(
        moments,
        [jax.ShapeDtypeStruct((3, chans, 3 * chans), F32)],
        (feat, *halo),
        "moments",
        18 * macs,
        56,
        [wide],
    )
    (parts,) = whole(
        finish,
        [jax.ShapeDtypeStruct((slides, 32, chans), F32)],
        (moment, point, taps),
        "finish",
        36 * chans * chans,
        32,
    )
    got = lax.all_to_all(parts, "slide", 0, 0, tiled=True)
    (feature_grad,) = whole(
        back,
        [jax.ShapeDtypeStruct((rows, cols, chans), BF16)],
        (*halo, point, taps),
        "back",
        18 * macs,
        56,
        [wide, pltpu.VMEM((3, chans, 3 * chans), BF16)],
    )
    (parts,) = whole(
        second,
        [jax.ShapeDtypeStruct((lax.axis_size(place), 16, chans), F32)],
        (got,),
        "second",
        1 << 20,
        16,
    )
    got = lax.all_to_all(parts, place, 0, 0, tiled=True)
    depth_grad, point_grad = whole(
        lambda *refs: third(scale, *refs),
        [jax.ShapeDtypeStruct((9, chans), F32), jax.ShapeDtypeStruct((1, chans), F32)],
        (got,),
        "third",
        1 << 20,
        16,
    )
    return feature_grad[None], point_grad, depth_grad


def solution(mesh):
    placed = (
        P("slide", "row", "col", None),
        P("slide", "row", "col", None),
        P(),
        P(("slide", "row", "col"), None),
    )
    return jax.shard_map(
        on_device,
        mesh=mesh,
        in_specs=placed,
        out_specs=(P("slide", "row", "col", None), P(("slide", "row", "col"), None), P()),
        check_vma=False,
    )
```

```python
import functools
import math

import jax
import jax.numpy as jnp
from jax import lax
from jax.experimental import pallas as pl
from jax.experimental.pallas import tpu as pltpu
from jax.sharding import PartitionSpec as P

BF16 = jnp.bfloat16
F32 = jnp.float32
IN_VMEM = pl.BlockSpec(memory_space=pltpu.VMEM)


def whole(body, outs, args, name, flops, limit, scratch=(), specs=None, alias=None):
    size = sum(math.prod(x.shape) * x.dtype.itemsize for x in (*args, *outs))
    ins, outs_at = specs or ([IN_VMEM] * len(args), [IN_VMEM] * len(outs))
    return pl.pallas_call(
        body,
        out_shape=outs,
        in_specs=ins,
        out_specs=outs_at,
        scratch_shapes=scratch,
        name=name,
        input_output_aliases=alias or {},
        cost_estimate=pl.CostEstimate(
            flops=flops, bytes_accessed=size, transcendentals=0
        ),
        compiler_params=pltpu.CompilerParams(vmem_limit_bytes=limit << 20),
    )(*args)


def prepare(row, grad, rows_out, top, bottom, lo, hi, first, last, sems):
    rows, cols, _ = grad.shape
    copies = [
        pltpu.make_async_copy(a, b, sems.at[n])
        for n, (a, b) in enumerate(
            (
                (grad.at[:, pl.ds(0, 8)], first),
                (grad.at[:, pl.ds(cols - 8, 8)], last),
                (grad.at[pl.ds(0, 2)], top),
                (grad.at[pl.ds(rows - 2, 2)], bottom),
            )
        )
    ]
    for copy in copies:
        copy.start()
    half = row.shape[1] // 2
    r = row[...].astype(F32)
    two = jnp.concatenate([r[:, :half], r[:, half:]], axis=0).astype(BF16)
    rows_out[...] = jnp.broadcast_to(two[None], rows_out.shape)
    for copy in copies:
        copy.wait()
    lo[...] = first[:, :2]
    hi[...] = last[:, 6:]


def ends(top, bottom, left, right, top_out, bottom_out):
    rows = left.shape[0]
    cols = top.shape[1]
    for out, part, at in ((top_out, top, 0), (bottom_out, bottom, rows - 2)):
        out[:, :cols] = part[...]
        fill = jnp.zeros((2, 4, left.shape[2]), BF16)
        out[:, cols:] = jnp.concatenate(
            [left[at : at + 2], right[at : at + 2], fill], axis=1
        )


def fetch(source, target, sems, bounds, offset):
    copies = [
        pltpu.make_async_copy(
            source.at[pl.ds(low, high - low)],
            target.at[pl.ds(low + offset, high - low)],
            sems.at[n],
        )
        for n, (low, high) in enumerate(zip(bounds, bounds[1:]))
    ]
    for copy in copies:
        copy.start()
    return copies


def each(low, high, body):
    lax.fori_loop(low, high, lambda i, c: (body(i), c)[1], 0)


def borders(above, below, left, right, rim, pair, sems):
    rows, cols = left.shape[0], above.shape[1] - 8
    copies = [
        pltpu.make_async_copy(x, to, sems.at[n])
        for n, (x, to) in enumerate(
            (
                (left, pair.at[0, pl.ds(2, rows)]),
                (right, pair.at[1, pl.ds(2, rows)]),
                (above, rim.at[0]),
                (below, rim.at[1]),
            )
        )
    ]
    for copy in copies:
        copy.start()
    for copy in copies:
        copy.wait()
    for n in range(2):
        at = slice(cols + 2 * n, cols + 2 * n + 2)
        pair[n, 0:2] = rim[0, :, at]
        pair[n, rows + 2 :] = rim[1, :, at]


def shift_rows(low, high, begin, grad, pair, wide):
    cols, chans = grad.shape[1:]

    def put(i):
        row = grad[i]
        wide[i, :, :chans] = jnp.concatenate([row[2:], pair[1, begin + i]], axis=0)
        wide[i, :, chans : 2 * chans] = row
        wide[i, :, 2 * chans :] = jnp.concatenate(
            [pair[0, begin + i], row[: cols - 2]], axis=0
        )

    each(low, high, put)


def four_products(feat, wide, first, fold):
    cols, chans = feat.shape[1:]
    lanes = wide.shape[2]
    fs, ds = [[], [], [], []], [[], [], [], []]
    for u in range(fold):
        i = first + 4 * u
        f0 = feat[pl.ds(i, 2)].reshape(2 * cols, chans)
        f1 = feat[pl.ds(i + 2, 2)].reshape(2 * cols, chans)
        d = [wide[pl.ds(i + 2 * k, 2)].reshape(2 * cols, lanes) for k in range(4)]
        for n, v in enumerate((f0, f0 + f1, f0 - f1, f1)):
            fs[n].append(v)
        for n, v in enumerate((d[0] - d[2], d[1] + d[2], d[1] - d[2], d[3] - d[1])):
            ds[n].append(v)
    return [
        lax.dot_general(
            jnp.concatenate(f, axis=0),
            jnp.concatenate(d, axis=0),
            (((0,), (0,)), ((), ())),
            preferred_element_type=F32,
        )
        for f, d in zip(fs, ds)
    ]


def products(
    blocks, fold, feat_hbm, grad_hbm, above, below, left, right, out,
    feat, grad, wide, rim, pair, feat_sems, grad_sems, rim_sems,
):
    rows, cols, _ = feat.shape
    edges = [sum(blocks[:n]) for n in range(len(blocks) + 1)]
    grads = fetch(
        grad_hbm, grad, grad_sems, [0, *(e + 2 for e in edges[1:-1]), rows], 2
    )
    feats = fetch(feat_hbm, feat, feat_sems, edges, 0)
    borders(above, below, left, right, rim, pair, rim_sems)
    grad[0:2] = rim[0, :, :cols]
    grad[rows + 2 :] = rim[1, :, :cols]
    made = 0
    for t, first in enumerate(edges[:-1]):
        grads[t].wait()
        feats[t].wait()
        shift_rows(made, edges[t + 1] + 4, 0, grad, pair, wide)
        made = edges[t + 1] + 4
        for i in range(first, edges[t + 1], 4 * fold):
            for n, v in enumerate(four_products(feat, wide, i, fold)):
                if i == 0:
                    out[n] = v
                else:
                    out[n] += v


def columns(taps):
    rows = jnp.zeros((128 - taps.shape[0], taps.shape[1]), F32)
    return jnp.concatenate([taps[...].astype(F32), rows], axis=0).T


def finish(prods, point, taps, out, whole_point, stage, sem):
    chans = point.shape[0]
    x = point[...].astype(F32)
    p = jnp.concatenate([x[:, 0], x[:, 1]], axis=1)
    whole_point[...] = p.astype(BF16)
    w = columns(taps)
    acc = jnp.zeros((chans, chans), F32)
    lane = lax.broadcasted_iota(jnp.int32, (chans, 128), 1)
    sums = jnp.zeros((chans, 128), F32)
    for b in range(3):
        at = slice(b * chans, (b + 1) * chans)
        one, two, three, four = (prods[n, :, at] for n in range(4))
        half = 0.5 * (two - three)
        for a, m in enumerate((four + half, 0.5 * (two + three), one + half)):
            k = 3 * a + b
            acc = acc + w[:, k : k + 1] * m
            sums = jnp.where(lane == k, jnp.sum(p * m, axis=1, keepdims=True), sums)
    groups = out.shape[0]
    share = chans // groups
    tap_rows = sums.T[:16]
    for s in range(groups):
        stage[s, :share] = acc[s * share : (s + 1) * share]
        stage[s, share:] = tap_rows
    copy = pltpu.make_async_copy(stage, out, sem)
    copy.start()
    copy.wait()


def second(got, done, out):
    del done
    total = got[0]
    for s in range(1, got.shape[0]):
        total = total + got[s]
    rows = total.shape[0] // 2
    tap = total[rows:]
    sub = lax.broadcasted_iota(jnp.int32, tap.shape, 0)
    for r in range(out.shape[0]):
        out[r] = jnp.where(sub == 9, total[r : r + 1], tap)


def third(scale, got, taps, row):
    total = got[0]
    for s in range(1, got.shape[0]):
        total = total + got[s]
    total = total * scale
    taps[...] = total[:9]
    row[...] = total[9:10]


def rows_back(
    begin, count, step, grad_hbm, above, below, left, right, weights, out,
    grad, wide, rim, pair, stage, grad_sems, rim_sems, out_sem,
):
    rows, cols, chans = out.shape
    low, high = max(begin - 2, 0), min(begin + count + 2, rows)
    waits = fetch(grad_hbm, grad, grad_sems, [low, high], 2 - begin)
    borders(above, below, left, right, rim, pair, rim_sems)
    if begin == 0:
        grad[0:2] = rim[0, :, :cols]
    if begin + count == rows:
        grad[count + 2 :] = rim[1, :, :cols]
    for copy in waits:
        copy.wait()
    shift_rows(0, count + 4, begin, grad, pair, wide)
    for t in range(0, count, step):
        acc = None
        for a in range(3):
            lhs = wide[pl.ds(t + 4 - 2 * a, step)]
            term = lax.dot_general(
                lhs.reshape(step * cols, 3 * chans),
                weights[a],
                (((1,), (1,)), ((), ())),
                preferred_element_type=F32,
            )
            acc = term if acc is None else acc + term
        stage[pl.ds(t, step)] = acc.reshape(step, cols, chans).astype(BF16)
    copy = pltpu.make_async_copy(stage, out.at[pl.ds(begin, count)], out_sem)
    copy.start()
    copy.wait()


def back_one(
    count, step, grad_hbm, above, below, left, right, point, taps, out, weights, done, *scratch
):
    chans = point.shape[0]
    p = point[...].astype(F32)
    w = columns(taps)
    for k in range(9):
        weights[k // 3, :, (k % 3) * chans : (k % 3 + 1) * chans] = (
            p * w[:, k : k + 1]
        ).astype(BF16)
    rows_back(
        0, count, step, grad_hbm, above, below, left, right, weights, out, *scratch
    )
    done[...] = jnp.zeros_like(done)


def back_two(
    begin, count, step, grad_hbm, above, below, left, right, weights, half, out, *scratch
):
    del half
    rows_back(
        begin, count, step, grad_hbm, above, below, left, right, weights, out, *scratch
    )


def moved(x, axis, by):
    count = lax.axis_size(axis)
    pairs = [(i, i + by) for i in range(count) if 0 <= i + by < count]
    return lax.ppermute(x, axis, pairs)


def swapped(x, axes):
    return lax.all_to_all(x, axes, 0, 0, tiled=True)


def on_device(features, out_grad, depth_weight, point_weight):
    stay = pltpu.with_memory_space_constraint
    feat, grad = (stay(x[0], pltpu.HBM) for x in (features, out_grad))
    rows, cols, chans = feat.shape
    place, every = ("row", "col"), ("slide", "row", "col")
    slides, places = lax.axis_size("slide"), lax.axis_size(place)
    scale = 1.0 / math.sqrt(slides * places * rows * cols)
    macs = rows * cols * chans * chans
    shape = jax.ShapeDtypeStruct
    hbm = pl.BlockSpec(memory_space=pltpu.HBM)
    vmem, dma = pltpu.VMEM, pltpu.SemaphoreType.DMA

    mine, top, bottom, lo, hi = whole(
        prepare,
        [
            shape((slides * places, 2, chans // 2), BF16),
            *[shape((2, cols, chans), BF16)] * 2,
            *[shape((rows, 2, chans), BF16)] * 2,
        ],
        (point_weight, grad),
        "prepare",
        1 << 20,
        4,
        [*[vmem((rows, 8, chans), BF16)] * 2, dma((4,))],
        ([IN_VMEM, hbm], [IN_VMEM] * 5),
    )
    point = swapped(mine, every)
    left = moved(hi, "col", 1)
    right = moved(lo, "col", -1)
    top, bottom = whole(
        ends,
        [shape((2, cols + 8, chans), BF16)] * 2,
        (top, bottom, left, right),
        "ends",
        1 << 10,
        2,
    )
    above = moved(bottom, "row", 1)
    below = moved(top, "row", -1)
    halo = (grad, *(stay(x, pltpu.HBM) for x in (above, below, left, right)))
    halo_specs = [hbm] * 5

    def buffers(count):
        return [
            vmem((count + 4, cols, chans), BF16),
            vmem((count + 4, cols, 3 * chans), BF16),
            vmem((2, 2, cols + 8, chans), BF16),
            vmem((2, rows + 4, 2, chans), BF16),
        ]

    blocks = (16, rows - 16)
    (prods,) = whole(
        functools.partial(products, blocks, 4),
        [shape((4, chans, 3 * chans), F32)],
        (feat, *halo),
        "products",
        12 * macs,
        46,
        [
            vmem((rows, cols, chans), BF16),
            *buffers(rows),
            *[dma((len(blocks),))] * 2,
            dma((4,)),
        ],
        ([hbm, *halo_specs], [IN_VMEM]),
    )
    parts, point = whole(
        finish,
        [pltpu.HBM((slides, 32, chans), F32), shape((chans, chans), BF16)],
        (prods, point, depth_weight),
        "finish",
        36 * chans * chans,
        8,
        [vmem((slides, 32, chans), F32), dma],
        ([IN_VMEM] * 3, [hbm, IN_VMEM]),
    )
    got = swapped(parts, "slide")

    early, step = 40, 8

    def scratch(count):
        return [
            *buffers(count),
            vmem((count, cols, chans), BF16),
            dma((1,)),
            dma((4,)),
            dma,
        ]

    half, weights, done = whole(
        functools.partial(back_one, early, step),
        [
            shape((rows, cols, chans), BF16),
            shape((3, chans, 3 * chans), BF16),
            shape((8, 128), F32),
        ],
        (*halo, point, depth_weight),
        "back_one",
        18 * macs * early // rows,
        40,
        scratch(early),
        ([*halo_specs, IN_VMEM, IN_VMEM], [hbm, IN_VMEM, IN_VMEM]),
    )
    (parts,) = whole(
        second, [shape((places, 16, chans), F32)], (got, done), "second", 1 << 20, 4
    )
    got = swapped(parts, place)
    (feature_grad,) = whole(
        functools.partial(back_two, early, rows - early, step),
        [shape((rows, cols, chans), BF16)],
        (*halo, weights, stay(half, pltpu.HBM)),
        "back_two",
        18 * macs * (rows - early) // rows,
        32,
        scratch(rows - early),
        ([*halo_specs, IN_VMEM, hbm], [hbm]),
        {6: 0},
    )
    depth_grad, point_grad = whole(
        functools.partial(third, scale),
        [shape((9, chans), F32), shape((1, chans), F32)],
        (got,),
        "third",
        1 << 20,
        4,
    )
    return feature_grad[None], point_grad, depth_grad


def solution(mesh):
    placed = (
        P("slide", "row", "col", None),
        P("slide", "row", "col", None),
        P(),
        P(("slide", "row", "col"), None),
    )
    return jax.shard_map(
        on_device,
        mesh=mesh,
        in_specs=placed,
        out_specs=(P("slide", "row", "col", None), P(("slide", "row", "col"), None), P()),
        check_vma=False,
    )
```

```python
import functools
import math

import jax
import jax.numpy as jnp
from jax import lax
from jax.experimental import pallas as pl
from jax.experimental.pallas import tpu as pltpu
from jax.sharding import PartitionSpec as P

BF16 = jnp.bfloat16
F32 = jnp.float32
IN_VMEM = pl.BlockSpec(memory_space=pltpu.VMEM)


def whole(body, outs, args, name, flops, limit, scratch=(), specs=None, alias=None):
    size = sum(math.prod(x.shape) * x.dtype.itemsize for x in (*args, *outs))
    ins, outs_at = specs or ([IN_VMEM] * len(args), [IN_VMEM] * len(outs))
    return pl.pallas_call(
        body,
        out_shape=outs,
        in_specs=ins,
        out_specs=outs_at,
        scratch_shapes=scratch,
        name=name,
        input_output_aliases=alias or {},
        cost_estimate=pl.CostEstimate(
            flops=flops, bytes_accessed=size, transcendentals=0
        ),
        compiler_params=pltpu.CompilerParams(vmem_limit_bytes=limit << 20),
    )(*args)


def either(flag, x, y):
    return jnp.where(flag, x, y), jnp.where(flag, y, x)


def prepare(weight, taps, grad, top, bottom, near, far, taps_out, first, last, row, sems):
    rows, cols, _ = grad.shape
    copies = [
        pltpu.make_async_copy(a, b, sems.at[n])
        for n, (a, b) in enumerate(
            (
                (grad.at[:, pl.ds(0, 8)], first),
                (grad.at[:, pl.ds(cols - 8, 8)], last),
                (weight, row),
                (taps, taps_out),
                (grad.at[pl.ds(0, 2)], top),
                (grad.at[pl.ds(rows - 2, 2)], bottom),
            )
        )
    ]
    for copy in copies:
        copy.start()
    for copy in copies:
        copy.wait()
    even = lax.axis_index("pair") == 0
    near[:rows], far[:rows] = either(even, last[:, 6:], first[:, :2])
    twice = jnp.broadcast_to(row[...].astype(F32), (2, row.shape[1])).astype(BF16)
    near[rows] = twice
    far[rows] = twice


def ends(
    mine, top, bottom, near, far, two_rows, near_out, far_out, left_out, right_out, side, sems
):
    rows = near.shape[0] - 1
    cols = top.shape[1]
    even = lax.axis_index("pair") == 0
    low, high = either(even, mine[rows].astype(F32), near[rows].astype(F32))
    pair = jnp.concatenate([low[:1], high[:1]], axis=0).astype(BF16)
    two_rows[...] = jnp.broadcast_to(pair[None], two_rows.shape)
    right, left = either(even, near[:rows], far[:rows])
    side[0], side[1] = left, right
    copies = [
        pltpu.make_async_copy(side.at[n], to, sems.at[n])
        for n, to in enumerate((left_out, right_out))
    ]
    for copy in copies:
        copy.start()
    fill = jnp.zeros((2, 4, near.shape[2]), BF16)
    upper, lower = (
        jnp.concatenate([left[at : at + 2], right[at : at + 2], fill], axis=1)
        for at in (0, rows - 2)
    )
    even = lax.rem(lax.axis_index("row"), 2) == 0
    near_out[:, :cols], far_out[:, :cols] = either(even, bottom[...], top[...])
    near_out[:, cols:], far_out[:, cols:] = either(even, lower, upper)
    for copy in copies:
        copy.wait()


def fetch(source, target, sems, bounds, offset):
    copies = [
        pltpu.make_async_copy(
            source.at[pl.ds(low, high - low)],
            target.at[pl.ds(low + offset, high - low)],
            sems.at[n],
        )
        for n, (low, high) in enumerate(zip(bounds, bounds[1:]))
    ]
    for copy in copies:
        copy.start()
    return copies


def each(low, high, body):
    lax.fori_loop(low, high, lambda i, c: (body(i), c)[1], 0)


def shift_rows(low, high, begin, grad, pair, wide):
    cols, chans = grad.shape[1:]

    def put(i):
        row = grad[i]
        wide[i, :, :chans] = jnp.concatenate([row[2:], pair[1, begin + i]], axis=0)
        wide[i, :, chans : 2 * chans] = row
        wide[i, :, 2 * chans :] = jnp.concatenate(
            [pair[0, begin + i], row[: cols - 2]], axis=0
        )

    each(low, high, put)


def four_products(feat, wide, first, fold):
    cols, chans = feat.shape[1:]
    lanes = wide.shape[2]
    fs, ds = [[], [], [], []], [[], [], [], []]
    for u in range(fold):
        i = first + 4 * u
        f0 = feat[pl.ds(i, 2)].reshape(2 * cols, chans)
        f1 = feat[pl.ds(i + 2, 2)].reshape(2 * cols, chans)
        d = [wide[pl.ds(i + 2 * k, 2)].reshape(2 * cols, lanes) for k in range(4)]
        for n, v in enumerate((f0, f0 + f1, f0 - f1, f1)):
            fs[n].append(v)
        for n, v in enumerate((d[0] - d[2], d[1] + d[2], d[1] - d[2], d[3] - d[1])):
            ds[n].append(v)
    return [
        lax.dot_general(
            jnp.concatenate(f, axis=0),
            jnp.concatenate(d, axis=0),
            (((0,), (0,)), ((), ())),
            preferred_element_type=F32,
        )
        for f, d in zip(fs, ds)
    ]


def products(
    blocks, fold, feat_hbm, grad_hbm, near_hbm, far_hbm, left, right,
    out, rim_out, pair_out, feat, grad, wide, pair, got, feat_sems, grad_sems, sems,
):
    rows, cols, _ = feat.shape
    edges = [sum(blocks[:n]) for n in range(len(blocks) + 1)]
    waits = [
        pltpu.make_async_copy(x, to, sems.at[3 + n])
        for n, (x, to) in enumerate(
            (
                (left, pair.at[0, pl.ds(2, rows)]),
                (right, pair.at[1, pl.ds(2, rows)]),
                (near_hbm, got.at[0]),
                (far_hbm, got.at[1]),
            )
        )
    ]
    for copy in waits:
        copy.start()
    grads = fetch(
        grad_hbm, grad, grad_sems, [0, *(e + 2 for e in edges[1:-1]), rows], 2
    )
    feats = fetch(feat_hbm, feat, feat_sems, edges, 0)
    for copy in waits:
        copy.wait()
    even = lax.rem(lax.axis_index("row"), 2) == 0
    below, above = either(even, got[0], got[1])
    for at, part in ((0, above), (rows + 2, below)):
        grad[at : at + 2] = part[:, :cols]
        for n in range(2):
            pair[n, at : at + 2] = part[:, cols + 2 * n : cols + 2 * n + 2]
    copies = [
        pltpu.make_async_copy(x, to, sems.at[n])
        for n, (x, to) in enumerate(
            (
                (grad.at[pl.ds(0, 2)], rim_out.at[0]),
                (grad.at[pl.ds(rows + 2, 2)], rim_out.at[1]),
                (pair, pair_out),
            )
        )
    ]
    for copy in copies:
        copy.start()
    made = 0
    for t, first in enumerate(edges[:-1]):
        grads[t].wait()
        feats[t].wait()
        shift_rows(made, edges[t + 1] + 4, 0, grad, pair, wide)
        made = edges[t + 1] + 4
        for i in range(first, edges[t + 1], 4 * fold):
            for n, v in enumerate(four_products(feat, wide, i, fold)):
                if i == 0:
                    out[n] = v
                else:
                    out[n] += v
    for copy in copies:
        copy.wait()


def columns(taps):
    rows = jnp.zeros((128 - taps.shape[0], taps.shape[1]), F32)
    return jnp.concatenate([taps[...].astype(F32), rows], axis=0).T


def finish(prods, point, taps, out, whole_point, stage, natural, sem):
    chans = taps.shape[1]
    x = point[...].astype(F32)
    lanes = natural.shape[2]
    for n in range(2):
        for h in range(2):
            part = x[:, n, h * lanes : (h + 1) * lanes]
            natural[h, pl.ds(n, chans // 2, stride=2)] = part
    p = jnp.concatenate([natural[0], natural[1]], axis=1)
    whole_point[...] = p.astype(BF16)
    w = columns(taps)
    acc = jnp.zeros((chans, chans), F32)
    lane = lax.broadcasted_iota(jnp.int32, (chans, 128), 1)
    sums = jnp.zeros((chans, 128), F32)
    for b in range(3):
        at = slice(b * chans, (b + 1) * chans)
        one, two, three, four = (prods[n, :, at] for n in range(4))
        half = 0.5 * (two - three)
        for a, m in enumerate((four + half, 0.5 * (two + three), one + half)):
            k = 3 * a + b
            acc = acc + w[:, k : k + 1] * m
            sums = jnp.where(lane == k, jnp.sum(p * m, axis=1, keepdims=True), sums)
    groups = out.shape[0]
    share = chans // groups
    tap_rows = sums.T[:16]
    for s in range(groups):
        stage[s, :share] = acc[s * share : (s + 1) * share]
        stage[s, share:] = tap_rows
    copy = pltpu.make_async_copy(stage, out, sem)
    copy.start()
    copy.wait()


def second(got, done, out):
    del done
    total = got[0]
    for s in range(1, got.shape[0]):
        total = total + got[s]
    rows = total.shape[0] // 2
    tap = total[rows:]
    sub = lax.broadcasted_iota(jnp.int32, tap.shape, 0)
    for r in range(out.shape[0]):
        out[r] = jnp.where(sub == 9, total[r : r + 1], tap)


def third(scale, got, taps, row):
    total = got[0]
    for s in range(1, got.shape[0]):
        total = total + got[s]
    total = total * scale
    taps[...] = total[:9]
    row[...] = total[9:10]


def rows_back(
    begin, count, step, grad_hbm, rim, pair_hbm, weights, out,
    grad, wide, pair, stage, sems,
):
    rows, cols, chans = out.shape
    low, high = max(begin - 2, 0), min(begin + count + 2, rows)
    parts = [(pair_hbm, pair)]
    if begin == 0:
        parts.append((rim.at[0], grad.at[pl.ds(0, 2)]))
    if begin + count == rows:
        parts.append((rim.at[1], grad.at[pl.ds(count + 2, 2)]))
    parts.append(
        (
            grad_hbm.at[pl.ds(low, high - low)],
            grad.at[pl.ds(low - begin + 2, high - low)],
        )
    )
    waits = [
        pltpu.make_async_copy(x, to, sems.at[n]) for n, (x, to) in enumerate(parts)
    ]
    for copy in waits:
        copy.start()
    weights = weights()
    for copy in waits:
        copy.wait()
    shift_rows(0, count + 4, begin, grad, pair, wide)
    for t in range(0, count, step):
        acc = None
        for a in range(3):
            lhs = wide[pl.ds(t + 4 - 2 * a, step)]
            term = lax.dot_general(
                lhs.reshape(step * cols, 3 * chans),
                weights[a],
                (((1,), (1,)), ((), ())),
                preferred_element_type=F32,
            )
            acc = term if acc is None else acc + term
        stage[pl.ds(t, step)] = acc.reshape(step, cols, chans).astype(BF16)
    copy = pltpu.make_async_copy(stage, out.at[pl.ds(begin, count)], sems.at[4])
    copy.start()
    copy.wait()


def back_one(
    count, step, grad_hbm, rim, pair_hbm, point, taps, out, weights, done, *scratch
):
    chans = point.shape[0]

    def scaled():
        p = point[...].astype(F32)
        w = columns(taps)
        for k in range(9):
            weights[k // 3, :, (k % 3) * chans : (k % 3 + 1) * chans] = (
                p * w[:, k : k + 1]
            ).astype(BF16)
        return weights

    rows_back(0, count, step, grad_hbm, rim, pair_hbm, scaled, out, *scratch)
    done[...] = jnp.zeros_like(done)


def back_two(
    begin, count, step, grad_hbm, rim, pair_hbm, weights, half, out, *scratch
):
    del half
    rows_back(
        begin, count, step, grad_hbm, rim, pair_hbm, lambda: weights, out, *scratch
    )


def across(near, far, axis):
    count = lax.axis_size(axis)
    pairs = [(i, i ^ 1) for i in range(count)]
    others = [(i, i + 1 if i % 2 else i - 1) for i in range(1, count - 1)]
    return lax.ppermute(near, axis, pairs), lax.ppermute(far, axis, others)


def swapped(x, axes):
    return lax.all_to_all(x, axes, 0, 0, tiled=True)


def on_device(features, out_grad, depth_weight, point_weight):
    stay = pltpu.with_memory_space_constraint
    feat, grad = (stay(x[0], pltpu.HBM) for x in (features, out_grad))
    rows, cols, chans = feat.shape
    col = ("half", "pair")
    place = ("row", *col)
    slides, places = lax.axis_size("slide"), lax.axis_size(place)
    scale = 1.0 / math.sqrt(slides * places * rows * cols)
    macs = rows * cols * chans * chans
    shape = jax.ShapeDtypeStruct
    hbm = pl.BlockSpec(memory_space=pltpu.HBM)
    vmem, dma = pltpu.VMEM, pltpu.SemaphoreType.DMA

    edge = shape((2, cols, chans), BF16)
    side = shape((rows + 1, 2, chans), BF16)
    top, bottom, near, far, taps = whole(
        prepare,
        [edge, edge, side, side, shape((9, chans), BF16)],
        (stay(point_weight, pltpu.HBM), stay(depth_weight, pltpu.HBM), grad),
        "prepare",
        1 << 20,
        4,
        [*[vmem((rows, 8, chans), BF16)] * 2, vmem((1, chans), BF16), dma((6,))],
        ([hbm] * 3, [IN_VMEM] * 5),
    )
    edge = shape((2, cols + 8, chans), BF16)
    two_rows, *edges, left, right = whole(
        ends,
        [
            shape((slides * places // 2, 2, chans), BF16),
            *[edge] * 2,
            *[pltpu.HBM((rows, 2, chans), BF16)] * 2,
        ],
        (near, top, bottom, *across(near, far, col)),
        "ends",
        1 << 10,
        3,
        [vmem((2, rows, 2, chans), BF16), dma((2,))],
        ([IN_VMEM] * 5, [IN_VMEM] * 3 + [hbm] * 2),
    )
    rims = across(*edges, "row")
    point = swapped(two_rows, ("slide", "row", "half"))

    def buffers(count):
        return [
            vmem((count + 4, cols, chans), BF16),
            vmem((count + 4, cols, 3 * chans), BF16),
            vmem((2, rows + 4, 2, chans), BF16),
        ]

    blocks = (16, rows - 16)
    prods, rim, pair = whole(
        functools.partial(products, blocks, 4),
        [
            shape((4, chans, 3 * chans), F32),
            pltpu.HBM((2, 2, cols, chans), BF16),
            pltpu.HBM((2, rows + 4, 2, chans), BF16),
        ],
        (feat, grad, *(stay(x, pltpu.HBM) for x in (*rims, left, right))),
        "products",
        12 * macs,
        46,
        [
            vmem((rows, cols, chans), BF16),
            *buffers(rows),
            vmem((2, 2, cols + 8, chans), BF16),
            *[dma((len(blocks),))] * 2,
            dma((7,)),
        ],
        ([hbm] * 6, [IN_VMEM, hbm, hbm]),
    )
    halo = [grad, *(stay(x, pltpu.HBM) for x in (rim, pair))]
    halo_specs = [hbm] * 3
    parts, point = whole(
        finish,
        [pltpu.HBM((slides, 32, chans), F32), shape((chans, chans), BF16)],
        (prods, point, taps),
        "finish",
        36 * chans * chans,
        8,
        [vmem((slides, 32, chans), F32), vmem((2, chans, chans // 2), F32), dma],
        ([IN_VMEM] * 3, [hbm, IN_VMEM]),
    )
    got = swapped(parts, "slide")

    early, step = 32, 8

    def scratch(count):
        return [
            *buffers(count),
            vmem((count, cols, chans), BF16),
            dma((5,)),
        ]

    half, weights, done = whole(
        functools.partial(back_one, early, step),
        [
            shape((rows, cols, chans), BF16),
            shape((3, chans, 3 * chans), BF16),
            shape((8, 128), F32),
        ],
        (*halo, point, taps),
        "back_one",
        18 * macs * early // rows,
        40,
        scratch(early),
        ([*halo_specs, IN_VMEM, IN_VMEM], [hbm, IN_VMEM, IN_VMEM]),
    )
    (parts,) = whole(
        second, [shape((places, 16, chans), F32)], (got, done), "second", 1 << 20, 4
    )
    got = swapped(parts, place)
    (feature_grad,) = whole(
        functools.partial(back_two, early, rows - early, step),
        [shape((rows, cols, chans), BF16)],
        (*halo, weights, stay(half, pltpu.HBM)),
        "back_two",
        18 * macs * (rows - early) // rows,
        32,
        scratch(rows - early),
        ([*halo_specs, IN_VMEM, hbm], [hbm]),
        {4: 0},
    )
    depth_grad, point_grad = whole(
        functools.partial(third, scale),
        [shape((9, chans), F32), shape((1, chans), F32)],
        (got,),
        "third",
        1 << 20,
        4,
    )
    return feature_grad[None], point_grad, depth_grad


def solution(mesh):
    slides, rows, cols = (mesh.shape[a] for a in ("slide", "row", "col"))
    fine = jax.sharding.Mesh(
        mesh.devices.reshape(slides, rows, cols // 2, 2), ("slide", "row", "half", "pair")
    )
    tiles = P("slide", "row", ("half", "pair"), None)
    lines = P(("slide", "row", "half", "pair"), None)
    return jax.shard_map(
        on_device,
        mesh=fine,
        in_specs=(tiles, tiles, P(), lines),
        out_specs=(tiles, lines, P()),
        check_vma=False,
    )
```

```python
import functools
import math

import jax
import jax.numpy as jnp
from jax import lax
from jax.experimental import pallas as pl
from jax.experimental.pallas import tpu as pltpu
from jax.sharding import PartitionSpec as P

BF16 = jnp.bfloat16
F32 = jnp.float32
IN_VMEM = pl.BlockSpec(memory_space=pltpu.VMEM)


def whole(body, outs, args, name, flops, limit, scratch=(), specs=None, alias=None):
    size = sum(math.prod(x.shape) * x.dtype.itemsize for x in (*args, *outs))
    ins, outs_at = specs or ([IN_VMEM] * len(args), [IN_VMEM] * len(outs))
    return pl.pallas_call(
        body,
        out_shape=outs,
        in_specs=ins,
        out_specs=outs_at,
        scratch_shapes=scratch,
        name=name,
        input_output_aliases=alias or {},
        cost_estimate=pl.CostEstimate(
            flops=flops, bytes_accessed=size, transcendentals=0
        ),
        compiler_params=pltpu.CompilerParams(vmem_limit_bytes=limit << 20),
    )(*args)


def either(flag, x, y):
    return jnp.where(flag, x, y), jnp.where(flag, y, x)


def prepare(weight, taps, grad, top, bottom, near, far, taps_out, first, last, row, sems):
    rows, cols, _ = grad.shape
    copies = [
        pltpu.make_async_copy(a, b, sems.at[n])
        for n, (a, b) in enumerate(
            (
                (grad.at[:, pl.ds(0, 8)], first),
                (grad.at[:, pl.ds(cols - 8, 8)], last),
                (weight, row),
                (taps, taps_out),
                (grad.at[pl.ds(0, 2)], top),
                (grad.at[pl.ds(rows - 2, 2)], bottom),
            )
        )
    ]
    for copy in copies:
        copy.start()
    for copy in copies:
        copy.wait()
    even = lax.axis_index("pair") == 0
    near[:rows], far[:rows] = either(even, last[:, 6:], first[:, :2])
    twice = jnp.broadcast_to(row[...].astype(F32), (2, row.shape[1])).astype(BF16)
    near[rows] = twice
    far[rows] = twice


def ends(
    mine, top, bottom, near, far, two_rows, near_out, far_out, left_out, right_out, side, sems
):
    rows = near.shape[0] - 1
    cols = top.shape[1]
    even = lax.axis_index("pair") == 0
    low, high = either(even, mine[rows].astype(F32), near[rows].astype(F32))
    pair = jnp.concatenate([low[:1], high[:1]], axis=0).astype(BF16)
    two_rows[...] = jnp.broadcast_to(pair[None], two_rows.shape)
    right, left = either(even, near[:rows], far[:rows])
    side[0], side[1] = left, right
    copies = [
        pltpu.make_async_copy(side.at[n], to, sems.at[n])
        for n, to in enumerate((left_out, right_out))
    ]
    for copy in copies:
        copy.start()
    fill = jnp.zeros((2, 4, near.shape[2]), BF16)
    upper, lower = (
        jnp.concatenate([left[at : at + 2], right[at : at + 2], fill], axis=1)
        for at in (0, rows - 2)
    )
    even = lax.rem(lax.axis_index("row"), 2) == 0
    near_out[:, :cols], far_out[:, :cols] = either(even, bottom[...], top[...])
    near_out[:, cols:], far_out[:, cols:] = either(even, lower, upper)
    for copy in copies:
        copy.wait()


def fetch(source, target, sems, bounds, offset):
    copies = [
        pltpu.make_async_copy(
            source.at[pl.ds(low, high - low)],
            target.at[pl.ds(low + offset, high - low)],
            sems.at[n],
        )
        for n, (low, high) in enumerate(zip(bounds, bounds[1:]))
    ]
    for copy in copies:
        copy.start()
    return copies


def each(low, high, body):
    lax.fori_loop(low, high, lambda i, c: (body(i), c)[1], 0)


def shift_rows(low, high, begin, grad, pair, wide):
    cols, chans = grad.shape[1:]

    def put(i):
        row = grad[i]
        wide[i, :, :chans] = jnp.concatenate([row[2:], pair[1, begin + i]], axis=0)
        wide[i, :, chans : 2 * chans] = row
        wide[i, :, 2 * chans :] = jnp.concatenate(
            [pair[0, begin + i], row[: cols - 2]], axis=0
        )

    each(low // 4, high // 4, lambda g: [put(4 * g + u) for u in range(4)])


def four_products(feat, wide, first, fold):
    cols, chans = feat.shape[1:]
    lanes = wide.shape[2]
    fs, ds = [[], [], [], []], [[], [], [], []]
    for u in range(fold):
        i = first + 4 * u
        f0 = feat[pl.ds(i, 2)].reshape(2 * cols, chans)
        f1 = feat[pl.ds(i + 2, 2)].reshape(2 * cols, chans)
        d = [wide[pl.ds(i + 2 * k, 2)].reshape(2 * cols, lanes) for k in range(4)]
        for n, v in enumerate((f0, f0 + f1, f0 - f1, f1)):
            fs[n].append(v)
        for n, v in enumerate((d[0] - d[2], d[1] + d[2], d[1] - d[2], d[3] - d[1])):
            ds[n].append(v)
    return [
        lax.dot_general(
            jnp.concatenate(f, axis=0),
            jnp.concatenate(d, axis=0),
            (((0,), (0,)), ((), ())),
            preferred_element_type=F32,
        )
        for f, d in zip(fs, ds)
    ]


def products(
    blocks, fold, feat_hbm, grad_hbm, near_hbm, far_hbm, left, right,
    out, rim_out, pair_out, feat, grad, wide, pair, got, feat_sems, grad_sems, sems,
):
    rows, cols, _ = feat.shape
    edges = [sum(blocks[:n]) for n in range(len(blocks) + 1)]
    waits = [
        pltpu.make_async_copy(x, to, sems.at[3 + n])
        for n, (x, to) in enumerate(
            (
                (left, pair.at[0, pl.ds(2, rows)]),
                (right, pair.at[1, pl.ds(2, rows)]),
                (near_hbm, got.at[0]),
                (far_hbm, got.at[1]),
            )
        )
    ]
    for copy in waits:
        copy.start()
    grads = fetch(
        grad_hbm, grad, grad_sems, [0, *(e + 2 for e in edges[1:-1]), rows], 2
    )
    feats = fetch(feat_hbm, feat, feat_sems, edges, 0)
    for copy in waits:
        copy.wait()
    even = lax.rem(lax.axis_index("row"), 2) == 0
    below, above = either(even, got[0], got[1])
    for at, part in ((0, above), (rows + 2, below)):
        grad[at : at + 2] = part[:, :cols]
        for n in range(2):
            pair[n, at : at + 2] = part[:, cols + 2 * n : cols + 2 * n + 2]
    copies = [
        pltpu.make_async_copy(x, to, sems.at[n])
        for n, (x, to) in enumerate(
            (
                (grad.at[pl.ds(0, 2)], rim_out.at[0]),
                (grad.at[pl.ds(rows + 2, 2)], rim_out.at[1]),
                (pair, pair_out),
            )
        )
    ]
    for copy in copies:
        copy.start()
    made = 0
    for t, first in enumerate(edges[:-1]):
        grads[t].wait()
        feats[t].wait()
        shift_rows(made, edges[t + 1] + 4, 0, grad, pair, wide)
        made = edges[t + 1] + 4
        for i in range(first, edges[t + 1], 4 * fold):
            for n, v in enumerate(four_products(feat, wide, i, fold)):
                if i == 0:
                    out[n] = v
                else:
                    out[n] += v
    for copy in copies:
        copy.wait()


def columns(taps):
    rows = jnp.zeros((128 - taps.shape[0], taps.shape[1]), F32)
    return jnp.concatenate([taps[...].astype(F32), rows], axis=0).T


def finish(prods, point, taps, out, whole_point, stage, natural, sem):
    chans = taps.shape[1]
    x = point[...].astype(F32)
    lanes = natural.shape[2]
    for n in range(2):
        for h in range(2):
            part = x[:, n, h * lanes : (h + 1) * lanes]
            natural[h, pl.ds(n, chans // 2, stride=2)] = part
    p = jnp.concatenate([natural[0], natural[1]], axis=1)
    whole_point[...] = p.astype(BF16)
    w = columns(taps)
    acc = jnp.zeros((chans, chans), F32)
    lane = lax.broadcasted_iota(jnp.int32, (chans, 128), 1)
    sums = jnp.zeros((chans, 128), F32)
    for b in range(3):
        at = slice(b * chans, (b + 1) * chans)
        one, two, three, four = (prods[n, :, at] for n in range(4))
        half = 0.5 * (two - three)
        for a, m in enumerate((four + half, 0.5 * (two + three), one + half)):
            k = 3 * a + b
            acc = acc + w[:, k : k + 1] * m
            sums = jnp.where(lane == k, jnp.sum(p * m, axis=1, keepdims=True), sums)
    groups = out.shape[0]
    share = chans // groups
    tap_rows = sums.T[:16]
    for s in range(groups):
        stage[s, :share] = acc[s * share : (s + 1) * share].astype(BF16)
        stage[s, share:] = tap_rows.astype(BF16)
    copy = pltpu.make_async_copy(stage, out, sem)
    copy.start()
    copy.wait()


def second(got, done, out):
    del done
    total = got[0].astype(F32)
    for s in range(1, got.shape[0]):
        total = total + got[s].astype(F32)
    rows = total.shape[0] // 2
    tap = total[rows:]
    sub = lax.broadcasted_iota(jnp.int32, tap.shape, 0)
    for r in range(out.shape[0]):
        out[r] = jnp.where(sub == 9, total[r : r + 1], tap)


def third(scale, got, taps, row):
    total = got[0]
    for s in range(1, got.shape[0]):
        total = total + got[s]
    total = total * scale
    taps[...] = total[:9]
    row[...] = total[9:10]


def rows_back(
    begin, count, step, grad_hbm, rim, pair_hbm, weights, out,
    grad, wide, pair, stage, sems,
):
    rows, cols, chans = out.shape
    low, high = max(begin - 2, 0), min(begin + count + 2, rows)
    parts = [(pair_hbm, pair)]
    if begin == 0:
        parts.append((rim.at[0], grad.at[pl.ds(0, 2)]))
    if begin + count == rows:
        parts.append((rim.at[1], grad.at[pl.ds(count + 2, 2)]))
    parts.append(
        (
            grad_hbm.at[pl.ds(low, high - low)],
            grad.at[pl.ds(low - begin + 2, high - low)],
        )
    )
    waits = [
        pltpu.make_async_copy(x, to, sems.at[n]) for n, (x, to) in enumerate(parts)
    ]
    for copy in waits:
        copy.start()
    weights = weights()
    for copy in waits:
        copy.wait()
    shift_rows(0, count + 4, begin, grad, pair, wide)
    for t in range(0, count, step):
        acc = None
        for a in range(3):
            lhs = wide[pl.ds(t + 4 - 2 * a, step)]
            term = lax.dot_general(
                lhs.reshape(step * cols, 3 * chans),
                weights[a],
                (((1,), (1,)), ((), ())),
                preferred_element_type=F32,
            )
            acc = term if acc is None else acc + term
        stage[pl.ds(t, step)] = acc.reshape(step, cols, chans).astype(BF16)
    copy = pltpu.make_async_copy(stage, out.at[pl.ds(begin, count)], sems.at[4])
    copy.start()
    copy.wait()


def back_one(
    count, step, grad_hbm, rim, pair_hbm, point, taps, out, weights, done, *scratch
):
    chans = point.shape[0]

    def scaled():
        p = point[...].astype(F32)
        w = columns(taps)
        for k in range(9):
            weights[k // 3, :, (k % 3) * chans : (k % 3 + 1) * chans] = (
                p * w[:, k : k + 1]
            ).astype(BF16)
        return weights

    rows_back(0, count, step, grad_hbm, rim, pair_hbm, scaled, out, *scratch)
    done[...] = jnp.zeros_like(done)


def back_two(
    begin, count, step, grad_hbm, rim, pair_hbm, weights, half, out, *scratch
):
    del half
    rows_back(
        begin, count, step, grad_hbm, rim, pair_hbm, lambda: weights, out, *scratch
    )


def across(near, far, axis):
    count = lax.axis_size(axis)
    pairs = [(i, i ^ 1) for i in range(count)]
    others = [(i, i + 1 if i % 2 else i - 1) for i in range(1, count - 1)]
    return lax.ppermute(near, axis, pairs), lax.ppermute(far, axis, others)


def swapped(x, axes):
    return lax.all_to_all(x, axes, 0, 0, tiled=True)


def on_device(features, out_grad, depth_weight, point_weight):
    stay = pltpu.with_memory_space_constraint
    feat, grad = (stay(x[0], pltpu.HBM) for x in (features, out_grad))
    rows, cols, chans = feat.shape
    col = ("half", "pair")
    place = ("row", *col)
    slides, places = lax.axis_size("slide"), lax.axis_size(place)
    scale = 1.0 / math.sqrt(slides * places * rows * cols)
    macs = rows * cols * chans * chans
    shape = jax.ShapeDtypeStruct
    hbm = pl.BlockSpec(memory_space=pltpu.HBM)
    vmem, dma = pltpu.VMEM, pltpu.SemaphoreType.DMA

    edge = shape((2, cols, chans), BF16)
    side = shape((rows + 1, 2, chans), BF16)
    top, bottom, near, far, taps = whole(
        prepare,
        [edge, edge, side, side, shape((9, chans), BF16)],
        (stay(point_weight, pltpu.HBM), stay(depth_weight, pltpu.HBM), grad),
        "prepare",
        1 << 20,
        4,
        [*[vmem((rows, 8, chans), BF16)] * 2, vmem((1, chans), BF16), dma((6,))],
        ([hbm] * 3, [IN_VMEM] * 5),
    )
    edge = shape((2, cols + 8, chans), BF16)
    two_rows, *edges, left, right = whole(
        ends,
        [
            shape((slides * places // 2, 2, chans), BF16),
            *[edge] * 2,
            *[pltpu.HBM((rows, 2, chans), BF16)] * 2,
        ],
        (near, top, bottom, *across(near, far, col)),
        "ends",
        1 << 10,
        3,
        [vmem((2, rows, 2, chans), BF16), dma((2,))],
        ([IN_VMEM] * 5, [IN_VMEM] * 3 + [hbm] * 2),
    )
    rims = across(*edges, "row")
    point = swapped(two_rows, ("slide", "row", "half"))

    def buffers(count):
        return [
            vmem((count + 4, cols, chans), BF16),
            vmem((count + 4, cols, 3 * chans), BF16),
            vmem((2, rows + 4, 2, chans), BF16),
        ]

    blocks = (16, rows - 16)
    prods, rim, pair = whole(
        functools.partial(products, blocks, 4),
        [
            shape((4, chans, 3 * chans), F32),
            pltpu.HBM((2, 2, cols, chans), BF16),
            pltpu.HBM((2, rows + 4, 2, chans), BF16),
        ],
        (feat, grad, *(stay(x, pltpu.HBM) for x in (*rims, left, right))),
        "products",
        12 * macs,
        46,
        [
            vmem((rows, cols, chans), BF16),
            *buffers(rows),
            vmem((2, 2, cols + 8, chans), BF16),
            *[dma((len(blocks),))] * 2,
            dma((7,)),
        ],
        ([hbm] * 6, [IN_VMEM, hbm, hbm]),
    )
    halo = [grad, *(stay(x, pltpu.HBM) for x in (rim, pair))]
    halo_specs = [hbm] * 3
    parts, point = whole(
        finish,
        [pltpu.HBM((slides, 32, chans), BF16), shape((chans, chans), BF16)],
        (prods, point, taps),
        "finish",
        36 * chans * chans,
        8,
        [vmem((slides, 32, chans), BF16), vmem((2, chans, chans // 2), F32), dma],
        ([IN_VMEM] * 3, [hbm, IN_VMEM]),
    )
    got = swapped(parts, "slide")

    early, step = 32, 8

    def scratch(count):
        return [
            *buffers(count),
            vmem((count, cols, chans), BF16),
            dma((5,)),
        ]

    half, weights, done = whole(
        functools.partial(back_one, early, step),
        [
            shape((rows, cols, chans), BF16),
            shape((3, chans, 3 * chans), BF16),
            shape((8, 128), F32),
        ],
        (*halo, point, taps),
        "back_one",
        18 * macs * early // rows,
        40,
        scratch(early),
        ([*halo_specs, IN_VMEM, IN_VMEM], [hbm, IN_VMEM, IN_VMEM]),
    )
    (parts,) = whole(
        second, [shape((places, 16, chans), F32)], (got, done), "second", 1 << 20, 4
    )
    got = swapped(parts, place)
    (feature_grad,) = whole(
        functools.partial(back_two, early, rows - early, step),
        [shape((rows, cols, chans), BF16)],
        (*halo, weights, stay(half, pltpu.HBM)),
        "back_two",
        18 * macs * (rows - early) // rows,
        32,
        scratch(rows - early),
        ([*halo_specs, IN_VMEM, hbm], [hbm]),
        {4: 0},
    )
    depth_grad, point_grad = whole(
        functools.partial(third, scale),
        [shape((9, chans), F32), shape((1, chans), F32)],
        (got,),
        "third",
        1 << 20,
        4,
    )
    return feature_grad[None], point_grad, depth_grad


def solution(mesh):
    slides, rows, cols = (mesh.shape[a] for a in ("slide", "row", "col"))
    fine = jax.sharding.Mesh(
        mesh.devices.reshape(slides, rows, cols // 2, 2), ("slide", "row", "half", "pair")
    )
    tiles = P("slide", "row", ("half", "pair"), None)
    lines = P(("slide", "row", "half", "pair"), None)
    return jax.shard_map(
        on_device,
        mesh=fine,
        in_specs=(tiles, tiles, P(), lines),
        out_specs=(tiles, lines, P()),
        check_vma=False,
    )
```

```python
import functools
import math

import jax
import jax.numpy as jnp
from jax import lax
from jax.experimental import pallas as pl
from jax.experimental.pallas import tpu as pltpu
from jax.sharding import PartitionSpec as P

BF16 = jnp.bfloat16
F32 = jnp.float32
IN_VMEM = pl.BlockSpec(memory_space=pltpu.VMEM)


def whole(body, outs, args, name, flops, limit, scratch=(), specs=None, alias=None):
    size = sum(math.prod(x.shape) * x.dtype.itemsize for x in (*args, *outs))
    ins, outs_at = specs or ([IN_VMEM] * len(args), [IN_VMEM] * len(outs))
    return pl.pallas_call(
        body,
        out_shape=outs,
        in_specs=ins,
        out_specs=outs_at,
        scratch_shapes=scratch,
        name=name,
        input_output_aliases=alias or {},
        cost_estimate=pl.CostEstimate(
            flops=flops, bytes_accessed=size, transcendentals=0
        ),
        compiler_params=pltpu.CompilerParams(vmem_limit_bytes=limit << 20),
    )(*args)


def either(flag, x, y):
    return jnp.where(flag, x, y), jnp.where(flag, y, x)


def prepare(weight, taps, grad, top, bottom, near, far, taps_out, first, last, row, sems):
    rows, cols, _ = grad.shape
    copies = [
        pltpu.make_async_copy(a, b, sems.at[n])
        for n, (a, b) in enumerate(
            (
                (grad.at[:, pl.ds(0, 8)], first),
                (grad.at[:, pl.ds(cols - 8, 8)], last),
                (weight, row),
                (taps, taps_out),
                (grad.at[pl.ds(0, 2)], top),
                (grad.at[pl.ds(rows - 2, 2)], bottom),
            )
        )
    ]
    for copy in copies:
        copy.start()
    for copy in copies:
        copy.wait()
    even = lax.axis_index("pair") == 0
    near[:rows], far[:rows] = either(even, last[:, 6:], first[:, :2])
    twice = jnp.broadcast_to(row[...].astype(F32), (2, row.shape[1])).astype(BF16)
    near[rows] = twice
    far[rows] = twice


def ends(
    mine, top, bottom, near, far, two_rows, near_out, far_out, left_out, right_out, side, sems
):
    rows = near.shape[0] - 1
    cols = top.shape[1]
    even = lax.axis_index("pair") == 0
    low, high = either(even, mine[rows].astype(F32), near[rows].astype(F32))
    pair = jnp.concatenate([low[:1], high[:1]], axis=0).astype(BF16)
    two_rows[...] = jnp.broadcast_to(pair[None], two_rows.shape)
    right, left = either(even, near[:rows], far[:rows])
    side[0], side[1] = left, right
    copies = [
        pltpu.make_async_copy(side.at[n], to, sems.at[n])
        for n, to in enumerate((left_out, right_out))
    ]
    for copy in copies:
        copy.start()
    fill = jnp.zeros((2, 4, near.shape[2]), BF16)
    upper, lower = (
        jnp.concatenate([left[at : at + 2], right[at : at + 2], fill], axis=1)
        for at in (0, rows - 2)
    )
    even = lax.rem(lax.axis_index("row"), 2) == 0
    near_out[:, :cols], far_out[:, :cols] = either(even, bottom[...], top[...])
    near_out[:, cols:], far_out[:, cols:] = either(even, lower, upper)
    for copy in copies:
        copy.wait()


def fetch(source, target, sems, bounds, offset):
    copies = [
        pltpu.make_async_copy(
            source.at[pl.ds(low, high - low)],
            target.at[pl.ds(low + offset, high - low)],
            sems.at[n],
        )
        for n, (low, high) in enumerate(zip(bounds, bounds[1:]))
    ]
    for copy in copies:
        copy.start()
    return copies


def each(low, high, body):
    lax.fori_loop(low, high, lambda i, c: (body(i), c)[1], 0)


def shift_rows(low, high, begin, grad, pair, wide):
    cols, chans = grad.shape[1:]

    def put(i):
        row = grad[i]
        wide[i, :, :chans] = jnp.concatenate([row[2:], pair[1, begin + i]], axis=0)
        wide[i, :, chans : 2 * chans] = row
        wide[i, :, 2 * chans :] = jnp.concatenate(
            [pair[0, begin + i], row[: cols - 2]], axis=0
        )

    each(low // 4, high // 4, lambda g: [put(4 * g + u) for u in range(4)])


def four_products(feat, wide, first, fold):
    cols, chans = feat.shape[1:]
    lanes = wide.shape[2]
    fs, ds = [[], [], [], []], [[], [], [], []]
    for u in range(fold):
        i = first + 4 * u
        f0 = feat[pl.ds(i, 2)].reshape(2 * cols, chans)
        f1 = feat[pl.ds(i + 2, 2)].reshape(2 * cols, chans)
        d = [wide[pl.ds(i + 2 * k, 2)].reshape(2 * cols, lanes) for k in range(4)]
        for n, v in enumerate((f0, f0 + f1, f0 - f1, f1)):
            fs[n].append(v)
        for n, v in enumerate((d[0] - d[2], d[1] + d[2], d[1] - d[2], d[3] - d[1])):
            ds[n].append(v)
    return [
        lax.dot_general(
            jnp.concatenate(f, axis=0),
            jnp.concatenate(d, axis=0),
            (((0,), (0,)), ((), ())),
            preferred_element_type=F32,
        )
        for f, d in zip(fs, ds)
    ]


def products(
    blocks, fold, feat_hbm, grad_hbm, near_hbm, far_hbm, left, right,
    out, rim_out, pair_out, feat, grad, wide, pair, got, feat_sems, grad_sems, sems,
):
    rows, cols, _ = feat.shape
    edges = [sum(blocks[:n]) for n in range(len(blocks) + 1)]
    waits = [
        pltpu.make_async_copy(x, to, sems.at[3 + n])
        for n, (x, to) in enumerate(
            (
                (left, pair.at[0, pl.ds(2, rows)]),
                (right, pair.at[1, pl.ds(2, rows)]),
                (near_hbm, got.at[0]),
                (far_hbm, got.at[1]),
            )
        )
    ]
    for copy in waits:
        copy.start()
    grads = fetch(
        grad_hbm, grad, grad_sems, [0, *(e + 2 for e in edges[1:-1]), rows], 2
    )
    feats = fetch(feat_hbm, feat, feat_sems, edges, 0)
    for copy in waits:
        copy.wait()
    even = lax.rem(lax.axis_index("row"), 2) == 0
    below, above = either(even, got[0], got[1])
    for at, part in ((0, above), (rows + 2, below)):
        grad[at : at + 2] = part[:, :cols]
        for n in range(2):
            pair[n, at : at + 2] = part[:, cols + 2 * n : cols + 2 * n + 2]
    copies = [
        pltpu.make_async_copy(x, to, sems.at[n])
        for n, (x, to) in enumerate(
            (
                (grad.at[pl.ds(0, 2)], rim_out.at[0]),
                (grad.at[pl.ds(rows + 2, 2)], rim_out.at[1]),
                (pair, pair_out),
            )
        )
    ]
    for copy in copies:
        copy.start()
    made = 0
    for t, first in enumerate(edges[:-1]):
        grads[t].wait()
        feats[t].wait()
        shift_rows(made, edges[t + 1] + 4, 0, grad, pair, wide)
        made = edges[t + 1] + 4
        for i in range(first, edges[t + 1], 4 * fold):
            for n, v in enumerate(four_products(feat, wide, i, fold)):
                if i == 0:
                    out[n] = v
                else:
                    out[n] += v
    for copy in copies:
        copy.wait()


def columns(taps):
    rows = jnp.zeros((128 - taps.shape[0], taps.shape[1]), F32)
    return jnp.concatenate([taps[...].astype(F32), rows], axis=0).T


def finish(prods, point, taps, out, whole_point, stage, natural, sem):
    chans = taps.shape[1]
    x = point[...].astype(F32)
    lanes = natural.shape[2]
    for n in range(2):
        for h in range(2):
            part = x[:, n, h * lanes : (h + 1) * lanes]
            natural[h, pl.ds(n, chans // 2, stride=2)] = part
    p = jnp.concatenate([natural[0], natural[1]], axis=1)
    whole_point[...] = p.astype(BF16)
    w = columns(taps)
    acc = jnp.zeros((chans, chans), F32)
    lane = lax.broadcasted_iota(jnp.int32, (chans, 128), 1)
    sums = jnp.zeros((chans, 128), F32)
    for b in range(3):
        at = slice(b * chans, (b + 1) * chans)
        one, two, three, four = (prods[n, :, at] for n in range(4))
        half = 0.5 * (two - three)
        for a, m in enumerate((four + half, 0.5 * (two + three), one + half)):
            k = 3 * a + b
            acc = acc + w[:, k : k + 1] * m
            sums = jnp.where(lane == k, jnp.sum(p * m, axis=1, keepdims=True), sums)
    groups = out.shape[0]
    share = chans // groups
    tap_rows = sums.T[:16]
    for s in range(groups):
        stage[s, :share] = acc[s * share : (s + 1) * share].astype(BF16)
        stage[s, share:] = tap_rows.astype(BF16)
    copy = pltpu.make_async_copy(stage, out, sem)
    copy.start()
    copy.wait()


def second(got, done, out):
    del done
    total = got[0].astype(F32)
    for s in range(1, got.shape[0]):
        total = total + got[s].astype(F32)
    rows = total.shape[0] // 2
    tap = total[rows:]
    sub = lax.broadcasted_iota(jnp.int32, tap.shape, 0)
    for r in range(out.shape[0]):
        out[r] = jnp.where(sub == 9, total[r : r + 1], tap).astype(BF16)


def third(scale, got, taps, row):
    total = got[0].astype(F32)
    for s in range(1, got.shape[0]):
        total = total + got[s].astype(F32)
    total = total * scale
    taps[...] = total[:9]
    row[...] = total[9:10]


def rows_back(
    begin, count, step, grad_hbm, rim, pair_hbm, weights, out,
    grad, wide, pair, stage, sems,
):
    rows, cols, chans = out.shape
    low, high = max(begin - 2, 0), min(begin + count + 2, rows)
    parts = [(pair_hbm, pair)]
    if begin == 0:
        parts.append((rim.at[0], grad.at[pl.ds(0, 2)]))
    if begin + count == rows:
        parts.append((rim.at[1], grad.at[pl.ds(count + 2, 2)]))
    parts.append(
        (
            grad_hbm.at[pl.ds(low, high - low)],
            grad.at[pl.ds(low - begin + 2, high - low)],
        )
    )
    waits = [
        pltpu.make_async_copy(x, to, sems.at[n]) for n, (x, to) in enumerate(parts)
    ]
    for copy in waits:
        copy.start()
    weights = weights()
    for copy in waits:
        copy.wait()
    shift_rows(0, count + 4, begin, grad, pair, wide)
    for t in range(0, count, step):
        acc = None
        for a in range(3):
            lhs = wide[pl.ds(t + 4 - 2 * a, step)]
            term = lax.dot_general(
                lhs.reshape(step * cols, 3 * chans),
                weights[a],
                (((1,), (1,)), ((), ())),
                preferred_element_type=F32,
            )
            acc = term if acc is None else acc + term
        stage[pl.ds(t, step)] = acc.reshape(step, cols, chans).astype(BF16)
    copy = pltpu.make_async_copy(stage, out.at[pl.ds(begin, count)], sems.at[4])
    copy.start()
    copy.wait()


def back_one(
    count, step, grad_hbm, rim, pair_hbm, point, taps, out, weights, done, *scratch
):
    chans = point.shape[0]

    def scaled():
        p = point[...].astype(F32)
        w = columns(taps)
        for k in range(9):
            weights[k // 3, :, (k % 3) * chans : (k % 3 + 1) * chans] = (
                p * w[:, k : k + 1]
            ).astype(BF16)
        return weights

    rows_back(0, count, step, grad_hbm, rim, pair_hbm, scaled, out, *scratch)
    done[...] = jnp.zeros_like(done)


def back_two(
    begin, count, step, grad_hbm, rim, pair_hbm, weights, half, out, *scratch
):
    del half
    rows_back(
        begin, count, step, grad_hbm, rim, pair_hbm, lambda: weights, out, *scratch
    )


def across(near, far, axis):
    count = lax.axis_size(axis)
    pairs = [(i, i ^ 1) for i in range(count)]
    others = [(i, i + 1 if i % 2 else i - 1) for i in range(1, count - 1)]
    return lax.ppermute(near, axis, pairs), lax.ppermute(far, axis, others)


def swapped(x, axes):
    return lax.all_to_all(x, axes, 0, 0, tiled=True)


def on_device(features, out_grad, depth_weight, point_weight):
    stay = pltpu.with_memory_space_constraint
    feat, grad = (stay(x[0], pltpu.HBM) for x in (features, out_grad))
    rows, cols, chans = feat.shape
    col = ("half", "pair")
    place = ("row", *col)
    slides, places = lax.axis_size("slide"), lax.axis_size(place)
    scale = 1.0 / math.sqrt(slides * places * rows * cols)
    macs = rows * cols * chans * chans
    shape = jax.ShapeDtypeStruct
    hbm = pl.BlockSpec(memory_space=pltpu.HBM)
    vmem, dma = pltpu.VMEM, pltpu.SemaphoreType.DMA

    edge = shape((2, cols, chans), BF16)
    side = shape((rows + 1, 2, chans), BF16)
    top, bottom, near, far, taps = whole(
        prepare,
        [edge, edge, side, side, shape((9, chans), BF16)],
        (stay(point_weight, pltpu.HBM), stay(depth_weight, pltpu.HBM), grad),
        "prepare",
        1 << 20,
        4,
        [*[vmem((rows, 8, chans), BF16)] * 2, vmem((1, chans), BF16), dma((6,))],
        ([hbm] * 3, [IN_VMEM] * 5),
    )
    edge = shape((2, cols + 8, chans), BF16)
    two_rows, *edges, left, right = whole(
        ends,
        [
            shape((slides * places // 2, 2, chans), BF16),
            *[edge] * 2,
            *[pltpu.HBM((rows, 2, chans), BF16)] * 2,
        ],
        (near, top, bottom, *across(near, far, col)),
        "ends",
        1 << 10,
        3,
        [vmem((2, rows, 2, chans), BF16), dma((2,))],
        ([IN_VMEM] * 5, [IN_VMEM] * 3 + [hbm] * 2),
    )
    rims = across(*edges, "row")
    point = swapped(two_rows, ("slide", "row", "half"))

    def buffers(count):
        return [
            vmem((count + 4, cols, chans), BF16),
            vmem((count + 4, cols, 3 * chans), BF16),
            vmem((2, rows + 4, 2, chans), BF16),
        ]

    blocks = (16, rows - 16)
    prods, rim, pair = whole(
        functools.partial(products, blocks, 4),
        [
            shape((4, chans, 3 * chans), F32),
            pltpu.HBM((2, 2, cols, chans), BF16),
            pltpu.HBM((2, rows + 4, 2, chans), BF16),
        ],
        (feat, grad, *(stay(x, pltpu.HBM) for x in (*rims, left, right))),
        "products",
        12 * macs,
        46,
        [
            vmem((rows, cols, chans), BF16),
            *buffers(rows),
            vmem((2, 2, cols + 8, chans), BF16),
            *[dma((len(blocks),))] * 2,
            dma((7,)),
        ],
        ([hbm] * 6, [IN_VMEM, hbm, hbm]),
    )
    halo = [grad, *(stay(x, pltpu.HBM) for x in (rim, pair))]
    halo_specs = [hbm] * 3
    parts, point = whole(
        finish,
        [pltpu.HBM((slides, 32, chans), BF16), shape((chans, chans), BF16)],
        (prods, point, taps),
        "finish",
        36 * chans * chans,
        8,
        [vmem((slides, 32, chans), BF16), vmem((2, chans, chans // 2), F32), dma],
        ([IN_VMEM] * 3, [hbm, IN_VMEM]),
    )
    got = swapped(parts, "slide")

    early, step = 32, 8

    def scratch(count):
        return [
            *buffers(count),
            vmem((count, cols, chans), BF16),
            dma((5,)),
        ]

    half, weights, done = whole(
        functools.partial(back_one, early, step),
        [
            shape((rows, cols, chans), BF16),
            shape((3, chans, 3 * chans), BF16),
            shape((8, 128), F32),
        ],
        (*halo, point, taps),
        "back_one",
        18 * macs * early // rows,
        40,
        scratch(early),
        ([*halo_specs, IN_VMEM, IN_VMEM], [hbm, IN_VMEM, IN_VMEM]),
    )
    (parts,) = whole(
        second, [shape((places, 16, chans), BF16)], (got, done), "second", 1 << 20, 4
    )
    got = swapped(parts, place)
    (feature_grad,) = whole(
        functools.partial(back_two, early, rows - early, step),
        [shape((rows, cols, chans), BF16)],
        (*halo, weights, stay(half, pltpu.HBM)),
        "back_two",
        18 * macs * (rows - early) // rows,
        32,
        scratch(rows - early),
        ([*halo_specs, IN_VMEM, hbm], [hbm]),
        {4: 0},
    )
    depth_grad, point_grad = whole(
        functools.partial(third, scale),
        [shape((9, chans), F32), shape((1, chans), F32)],
        (got,),
        "third",
        1 << 20,
        4,
    )
    return feature_grad[None], point_grad, depth_grad


def solution(mesh):
    slides, rows, cols = (mesh.shape[a] for a in ("slide", "row", "col"))
    fine = jax.sharding.Mesh(
        mesh.devices.reshape(slides, rows, cols // 2, 2), ("slide", "row", "half", "pair")
    )
    tiles = P("slide", "row", ("half", "pair"), None)
    lines = P(("slide", "row", "half", "pair"), None)
    return jax.shard_map(
        on_device,
        mesh=fine,
        in_specs=(tiles, tiles, P(), lines),
        out_specs=(tiles, lines, P()),
        check_vma=False,
    )
```
